32 devices in a mesh: grp: 2 (over core), gx: 4 (over z), gy: 4 (over y, x).
Axes of the slice: x: 2, y: 2, z: 4, core: 2. Of those that a mesh axis runs over, the one named last changes fastest.
Arguments:
- fields: float32 [2, 3, 128, 512], P('grp', None, 'gx', 'gy'), may hold values from -6 to 6
- coefficients: float32 [2, 128, 512], P('grp', 'gx', 'gy'), may hold values from 0.05 to 0.24
- forcing: float32 [2, 3, 128, 512], P('grp', None, 'gx', 'gy'), may hold values from -4 to 4
- element_matrix: float32 [12, 12], replicated, as said below
- source_cells: int32 [2, 1024, 128], P('grp', ('gx', 'gy')), may hold values from 0 to 4095
- target_cells: int32 [2, 1024, 128], P('grp', ('gx', 'gy')), may hold values from 0 to 4095
- peer_map: int32 [2, 1024, 1], P('grp', ('gx', 'gy')), may hold values from 0 to 15; in each aligned block of 64 rows (0 to 63, 64 to 127, ..., all dimensions but the last counted through in order) at most 8 rows name the same one
- mapping_blocks: bfloat16 [2, 1024, 128, 128], P('grp', ('gx', 'gy')), may hold values from -0.25 to 0.25
Outputs:
- new_fields: float32 [2, 3, 128, 512], P('grp', None, 'gx', 'gy')
- interface_load: float32 [2, 3, 128, 512], P('grp', None, 'gx', 'gy')
The draws below stay inside these ranges and needn't reach their ends.
Inputs may be any that keep to these rules, and one draw needn't show every extreme that they name: `peer_map`: within the 64 blocks of one partition no receiving partition is named more than 8 times. `source_cells`: local point indices of the sending partition. `target_cells`: local point indices of the receiving partition. `element_matrix`: Symmetric; every diagonal entry exceeds the sum of magnitudes of the other entries of its row by 0.5 or more.
All inputs are finite; a program needn't handle non-finite values.
Results may differ from the reference program's by a relative error of at most 0.012.
Values sent between devices are 32-bit elements; how exact they have to be, the bound alone decides.
A program may use at most 128 MiB of HBM per device.

```python
import math
import jax
import jax.numpy as jnp
import numpy as np
from jax import lax

CX = 32
CY = 128
NBLK = 64
BLOCK = 128
ITERS = 4
SUB = 4
PARTS_SIZE = 16
CAP = 8
NX = 128
NY = 512
N_GX = 4
N_GY = 4


def draw_element_matrix(key, part):
    first, second = jax.random.split(jax.random.fold_in(key, 11))
    rough = jax.random.normal(first, (12, 12), jnp.float32) * 0.25
    symmetric = 0.5 * (rough + rough.T)
    offdiag = symmetric * (1.0 - jnp.eye(12, dtype=jnp.float32))
    margin = jax.random.uniform(second, (12,), jnp.float32, 0.5, 1.5)
    return offdiag + jnp.diag(jnp.sum(jnp.abs(offdiag), axis=1) + margin)


def touch_ends(result, key, low, top_value):
    longest = result.shape.index(max(result.shape))
    spots = []
    for shift in (0, 1):
        where = [jax.random.randint(jax.random.fold_in(key, axis), (), 0, length) for axis, length in enumerate(result.shape)]
        where[longest] = (where[longest] + shift) % result.shape[longest]
        spots.append(tuple(where))
    return result.at[spots[0]].set(low).at[spots[1]].set(top_value)


def steps_of(stream_key, dims, cuts, smallest, largest):
    factor_of, own = 1.0, jax.random.fold_in(stream_key, 6)
    for axis_at, parts in cuts:
        heights = jnp.exp(jax.random.uniform(jax.random.fold_in(own, axis_at), (parts,), jnp.float32, smallest / len(cuts), largest / len(cuts)))
        factor_of = factor_of * jnp.repeat(heights, dims[axis_at] // parts).reshape([-1 if axis == axis_at else 1 for axis in range(len(dims))])
    return factor_of


def deal_out(own_key, own, number, rows, count, top, most, skew):
    ranking = jax.random.permutation(own_key, count)
    crowded, ordinary = shares(count, rows * top, most, skew, True), shares(count, rows * top, most, skew, False)
    places = jnp.arange(count)

    def named(sizes, turn):
        used = int((sizes > 0).sum())
        fixed = max(1, used // 4)
        passed = fixed + (places - fixed + turn * (used - fixed)) % max(1, count - fixed)
        return jnp.zeros((count,), jnp.int32).at[ranking[jnp.where(places < fixed, places, passed)]].set(jnp.asarray(sizes, jnp.int32))

    sizes = jnp.where(number % 4 == 0, named(crowded, number // 4), named(ordinary, number - number // 4 - 1))
    mixed = jax.random.permutation(jax.random.fold_in(own, 3), count)
    source_of, receiver = mixed[0:count // 2 * 2:2], mixed[1:count // 2 * 2:2]
    room = jnp.minimum(sizes[source_of] - 1, most - sizes[receiver]) // 2
    room = jnp.where((source_of == ranking[0]) | (receiver == ranking[0]) | (sizes[receiver] == 0), 0, jnp.maximum(room, 0))
    passed = jax.random.randint(jax.random.fold_in(own, 4), (count // 2,), 0, 1 << 20) % (room + 1)
    sizes = sizes.at[source_of].add(-passed).at[receiver].add(passed)
    items = jnp.searchsorted(jnp.cumsum(sizes), jnp.arange(rows * top), side="right").astype(jnp.int32)
    grid = items.reshape(top, rows).T
    grid = grid[jax.random.permutation(jax.random.fold_in(own, 1), rows)]
    turn = jax.random.randint(jax.random.fold_in(own, 2), (rows, 1), 0, top)
    return jnp.take_along_axis(grid, (jnp.arange(top)[None, :] + turn) % top, axis=1)


def shares(amount, total, reach, skew, full):
    loads = [(1 << 20) // math.isqrt(rank ** skew) + 1 for rank in range(1, amount + 1)]
    largest = reach if full else min(reach, max(-(-total // amount), total * loads[0] // sum(loads)))
    least = 1 if total - largest >= amount - 1 else 0
    counts, spare = [largest] + [least] * (amount - 1), total - largest - least * (amount - 1)
    while spare > 0:
        free = [i for i in range(1, amount) if counts[i] < largest] or [i for i in range(1, amount) if counts[i] < reach]
        mass, left = sum([loads[i] for i in free]), spare
        for i in free:
            addition = min(reach - counts[i], max(1, left * loads[i] // mass), spare)
            counts[i] = counts[i] + addition
            spare = spare - addition
    return np.array(counts)


def noise(stream_key, extent, deviation, limit, cuts=(), kind=jnp.bfloat16):
    factor_of = steps_of(stream_key, extent, cuts, -0.22, 0.18) if cuts else 1.0
    values = jax.random.normal(stream_key, extent, jnp.float32) * deviation * factor_of
    return jnp.minimum(jnp.maximum(values, -limit), limit).astype(kind)


def setup_inputs(seed: int = 0) -> dict:
    key_of = jax.random.split(jax.random.key(seed), 9)
    fields = noise(key_of[0], (2, 3, NX, NY), 1.0, 6.0, ((0, 2), (2, 4), (3, 4)), jnp.float32)
    coefficients = jnp.clip(jnp.exp(math.log(0.24) - 1.5686159 * jax.random.uniform(key_of[1], (2, NX, NY), jnp.float32) ** steps_of(key_of[1], (2, NX, NY), ((0, 2), (1, 4), (2, 4)), -0.2, 0.2)), 0.05, 0.24)
    forcing = noise(key_of[2], (2, 3, NX, NY), 0.3, 4.0, ((0, 2), (2, 4), (3, 4)), jnp.float32)
    element_matrix = draw_element_matrix(jax.random.fold_in(key_of[8], 71), 0)
    source_cells = touch_ends(jax.random.randint(key_of[4], (2, PARTS_SIZE * NBLK, BLOCK), 0, CX * CY), jax.random.fold_in(key_of[4], 1), 0, (CX * CY) - 1).astype(jnp.int32)
    target_cells = touch_ends(jax.random.randint(key_of[5], (2, PARTS_SIZE * NBLK, BLOCK), 0, CX * CY), jax.random.fold_in(key_of[5], 1), 0, (CX * CY) - 1).astype(jnp.int32)
    peer_map_keys = jax.random.split(jax.random.fold_in(key_of[6], 1), 2 * (PARTS_SIZE * NBLK) // NBLK)
    peer_map_turns = jax.random.permutation(jax.random.fold_in(key_of[6], 3), 2 * (PARTS_SIZE * NBLK) // NBLK)
    peer_map = jax.vmap(lambda own, number: deal_out(jax.random.fold_in(key_of[6], 2), own, number, NBLK, N_GX * N_GY, 1, CAP, 2))(peer_map_keys, peer_map_turns).reshape((2, PARTS_SIZE * NBLK, 1))
    mapping_blocks = noise(key_of[7], (2, PARTS_SIZE * NBLK, BLOCK, BLOCK), (4 * BLOCK) ** -0.5, 0.25, ((0, 2), (1, 16)))
    return dict(fields=fields, coefficients=coefficients, forcing=forcing, element_matrix=element_matrix, source_cells=source_cells, target_cells=target_cells, peer_map=peer_map, mapping_blocks=mapping_blocks)


DT_STEP = 1.0
RELAX = 0.6


def fluid_sweep(padded, viscous, forcing, applied):
    centre = padded[:, 1:-1, 1:-1]
    middle = viscous[1:-1, 1:-1]
    flux_sum = 0.5 * (middle + viscous[2:, 1:-1]) * (padded[:, 2:, 1:-1] - centre)
    flux_sum = flux_sum + 0.5 * (middle + viscous[:-2, 1:-1]) * (padded[:, :-2, 1:-1] - centre)
    flux_sum = flux_sum + 0.5 * (middle + viscous[1:-1, 2:]) * (padded[:, 1:-1, 2:] - centre)
    flux_sum = flux_sum + 0.5 * (middle + viscous[1:-1, :-2]) * (padded[:, 1:-1, :-2] - centre)
    return centre + DT_STEP * (flux_sum + forcing + applied)


def shell_sweep(padded, stiff_pad, element_matrix, forcing, applied):
    stiffness = stiff_pad[:-1, :-1]
    nodal = jnp.concatenate([padded[:, :-1, :-1], padded[:, 1:, :-1], padded[:, :-1, 1:], padded[:, 1:, 1:]], axis=0)
    element_force = jnp.einsum("ab,bxy->axy", element_matrix, nodal, precision=lax.Precision.HIGHEST) * stiffness
    nodal_force = element_force[0:3, 1:, 1:] + element_force[3:6, :-1, 1:]
    nodal_force = nodal_force + element_force[6:9, 1:, :-1] + element_force[9:12, :-1, :-1]
    diag_terms = jnp.diagonal(element_matrix)
    diagonal = diag_terms[0:3, None, None] * stiffness[None, 1:, 1:] + diag_terms[3:6, None, None] * stiffness[None, :-1, 1:]
    diagonal = diagonal + diag_terms[6:9, None, None] * stiffness[None, 1:, :-1] + diag_terms[9:12, None, None] * stiffness[None, :-1, :-1]
    return padded[:, 1:-1, 1:-1] + RELAX * (forcing + applied - nodal_force) / diagonal


def blocks_of(values):
    comps = values.shape[0]
    shaped = values.reshape(comps, N_GX, CX, N_GY, CY).transpose(1, 3, 0, 2, 4)
    return shaped.reshape(N_GX * N_GY, comps, CX * CY)


def grid_of(blocks):
    comps = blocks.shape[1]
    shaped = blocks.reshape(N_GX, N_GY, comps, CX, CY).transpose(2, 0, 3, 1, 4)
    return shaped.reshape(comps, CX * N_GX, CY * N_GY)


def outgoing(values, source_cells, mapping_blocks):
    partitions = N_GX * N_GY
    parted = blocks_of(values)

    def per_part(pieces):
        local, cells, matrices = pieces
        read = local[:, cells].astype(jnp.bfloat16).astype(jnp.float32)
        return jnp.einsum("cln,lnm->lcm", read, matrices.astype(jnp.float32))

    mapped = lax.map(per_part, (parted, source_cells.reshape(partitions, NBLK, BLOCK), mapping_blocks.reshape(partitions, NBLK, BLOCK, BLOCK)))
    return mapped.reshape(partitions * NBLK, 3, BLOCK)


def incoming(mapped, peer_map, target_cells):
    partitions = N_GX * N_GY
    where = (peer_map[:, 0:1] * (CX * CY) + target_cells).astype(jnp.int32)
    flat = jnp.zeros((3, partitions * CX * CY), jnp.float32)
    flat = flat.at[:, where.reshape(-1)].add(mapped.transpose(1, 0, 2).reshape(3, -1))
    return grid_of(flat.reshape(3, partitions, CX * CY).transpose(1, 0, 2))


def reference(fields, coefficients, forcing, element_matrix, source_cells, target_cells, peer_map, mapping_blocks):
    fluid_field = fields[0]
    shell_field = fields[1]
    viscous = jnp.pad(coefficients[0], 1)
    stiff_pad = jnp.pad(coefficients[1], 1)
    applied = jnp.zeros((2, 3, CX * N_GX, CY * N_GY), jnp.float32)
    edges = ((0, 0), (1, 1), (1, 1))
    for outer in range(ITERS):
        for inner in range(SUB):
            fluid_field = fluid_sweep(jnp.pad(fluid_field, edges), viscous, forcing[0], applied[0])
            shell_field = shell_sweep(jnp.pad(shell_field, edges), stiff_pad, element_matrix, forcing[1], applied[1])
        to_shell = incoming(outgoing(fluid_field, source_cells[0], mapping_blocks[0]), peer_map[0], target_cells[0])
        to_fluid = incoming(outgoing(shell_field, source_cells[1], mapping_blocks[1]), peer_map[1], target_cells[1])
        applied = jnp.stack([to_fluid, to_shell])
    return jnp.stack([fluid_field, shell_field]), applied
```

```python
import functools

import jax
import jax.numpy as jnp
from jax import lax
from jax.experimental import pallas as pl
from jax.experimental.pallas import tpu as pltpu
from jax.sharding import PartitionSpec as P

ITERS = 4
SUB = 4
DT_STEP = 1.0
RELAX = 0.6
ROWS = 8
LANES = 128
F32 = jnp.float32
BF16 = jnp.bfloat16


def iota(shape, dim):
    return lax.broadcasted_iota(jnp.int32, shape, dim)


def shift(value, amount, axis):
    return pltpu.roll(value, amount % value.shape[axis], axis)


def one_hot(mask):
    return jnp.where(mask, 1.0, 0.0).astype(BF16)


def flat_rows(block):
    return jnp.concatenate([block[k : k + 1] for k in range(block.shape[0])], axis=1)


def kernel(
    parts_x,
    parts_y,
    field_ref,
    coef_ref,
    force_ref,
    element_ref,
    source_ref,
    target_ref,
    peer_ref,
    map_ref,
    field_out,
    load_out,
    state,
    load,
    stat,
    row_send,
    col_send,
    row_recv,
    col_recv,
    corner_recv,
    spread,
    slot_map,
    value_send,
    value_recv,
    index_send,
    index_recv,
    halo_ss,
    halo_rs,
    value_ss,
    value_rs,
    index_ss,
    index_rs,
):
    comps, cells_x, cells_y = field_ref.shape[1:]
    links, width = source_ref.shape[1:]
    parts = parts_x * parts_y
    slots = parts * ROWS
    ext_x, ext_y = state.shape[1:]
    group = lax.axis_index("grp")
    gx = lax.axis_index("gx")
    gy = lax.axis_index("gy")
    me = gx * parts_y + gy

    def peer_device(q):
        return {"grp": 1 - group, "gx": lax.div(q, parts_y), "gy": lax.rem(q, parts_y)}

    def inside(dx, dy):
        ok = None
        for pos, step, size in ((gx, dx, parts_x), (gy, dy, parts_y)):
            if step:
                test = (pos + step >= 0) & (pos + step < size)
                ok = test if ok is None else ok & test
        return ok

    steps = ((1, 0), (-1, 0), (0, -1), (0, 1), (-1, -1), (-1, 1), (1, -1), (1, 1))

    row_send[...] = jnp.zeros_like(row_send)
    col_send[...] = jnp.zeros_like(col_send)
    row_recv[...] = jnp.zeros_like(row_recv)
    col_recv[...] = jnp.zeros_like(col_recv)
    corner_recv[...] = jnp.zeros_like(corner_recv)

    barrier = pltpu.get_barrier_semaphore()

    def greet(k, carry):
        q = lax.rem(me + k, parts)
        pl.semaphore_signal(
            barrier, inc=1, device_id=peer_device(q), device_id_type=pl.DeviceIdType.MESH
        )
        return carry

    lax.fori_loop(0, parts, greet, 0)
    for dx, dy in steps:

        @pl.when(inside(dx, dy))
        def _(dx=dx, dy=dy):
            pl.semaphore_signal(
                barrier,
                inc=1,
                device_id={"gx": gx + dx, "gy": gy + dy},
                device_id_type=pl.DeviceIdType.MESH,
            )

    beside_x = jnp.where(gx > 0, 1, 0) + jnp.where(gx < parts_x - 1, 1, 0)
    beside_y = jnp.where(gy > 0, 1, 0) + jnp.where(gy < parts_y - 1, 1, 0)
    pl.semaphore_wait(barrier, parts + (beside_x + 1) * (beside_y + 1) - 1)

    peer_col = jnp.broadcast_to(peer_ref[0].astype(F32), (links, links))
    above, across = iota((links, links), 0), iota((links, links), 1)
    peer_row = jnp.sum(jnp.where(above == across, peer_col, 0.0), axis=0, keepdims=True)
    rank = jnp.sum(
        jnp.where((peer_col == peer_row) & (above < across), 1.0, 0.0), axis=0, keepdims=True
    )
    slot_row = (peer_row * ROWS + rank).astype(jnp.int32)
    to_slot = one_hot(iota((slots, links), 0) == slot_row)
    repeat = one_hot(iota((links, links * ROWS), 0) == iota((links, links * ROWS), 1) // ROWS)
    slot_map[...] = jnp.dot(to_slot, repeat, preferred_element_type=F32).astype(BF16)
    target = target_ref[0]
    target_x = (target // cells_y).astype(F32).astype(BF16)
    target_y = (target % cells_y).astype(F32).astype(BF16)
    index = cells_y * jnp.dot(to_slot, target_x, preferred_element_type=F32)
    index = index + jnp.dot(to_slot, target_y, preferred_element_type=F32)
    index_send[...] = index.reshape(parts, ROWS, width)

    def index_copy(q, owner):
        return pltpu.make_async_remote_copy(
            src_ref=index_send.at[q],
            dst_ref=index_recv.at[owner],
            send_sem=index_ss.at[q],
            recv_sem=index_rs.at[owner],
            device_id=peer_device(q),
            device_id_type=pl.DeviceIdType.MESH,
        )

    def value_copy(q, owner, par):
        return pltpu.make_async_remote_copy(
            src_ref=value_send.at[q],
            dst_ref=value_recv.at[par, owner],
            send_sem=value_ss.at[q],
            recv_sem=value_rs.at[par, owner],
            device_id=peer_device(q),
            device_id_type=pl.DeviceIdType.MESH,
        )

    def halo_copy(d, par):
        dx, dy = steps[d]
        if d < 2:
            source, place = row_send.at[1 - d], row_recv.at[par, d]
        elif d < 4:
            source, place = col_send, col_recv.at[par, d - 2]
        else:
            edge = pl.ds(0, ROWS) if d < 6 else pl.ds(cells_x - ROWS, ROWS)
            source, place = col_send.at[edge], corner_recv.at[par, d - 4]
        return pltpu.make_async_remote_copy(
            src_ref=source,
            dst_ref=place,
            send_sem=halo_ss.at[d],
            recv_sem=halo_rs.at[par, d],
            device_id={"gx": gx + dx, "gy": gy + dy},
            device_id_type=pl.DeviceIdType.MESH,
        )

    def send_index(k, carry):
        index_copy(lax.rem(me + k, parts), me).start()
        return carry

    lax.fori_loop(0, parts, send_index, 0)

    for c in range(comps):
        state[c, :cells_x, :cells_y] = field_ref[0, c]
        load[c, :cells_x, :cells_y] = force_ref[0, c]

    ext_row = iota((ext_x, ext_y), 0)
    ext_col = iota((ext_x, ext_y), 1)
    row_at = jnp.where(ext_row < cells_x + SUB, ext_row, ext_row - ext_x) + gx * cells_x
    near = (ext_col < cells_y + SUB) | (ext_col >= ext_y - SUB)
    col_at = jnp.where(ext_col < cells_y + SUB, ext_col, ext_col - ext_y) + gy * cells_y
    keep = near & (row_at >= 0) & (row_at < cells_x * parts_x)
    keep = keep & (col_at >= 0) & (col_at < cells_y * parts_y)

    def coupling(t, carry):
        par = lax.rem(t, 2)
        centres = [state[c, :cells_x, :cells_y] for c in range(comps)]
        centres += [load[c, :cells_x, :cells_y] for c in range(comps)]
        centres.append(coef_ref[0])
        lane = iota((cells_x, cells_y), 1)
        packed = jnp.zeros((cells_x, cells_y), F32)
        for q, centre in enumerate(centres):
            row_send[0, q] = centre[:ROWS]
            row_send[1, q] = centre[cells_x - ROWS :]
            low = (lane >= 8 * q) & (lane < 8 * q + 4)
            high = (lane >= 8 * q + 4) & (lane < 8 * q + 8)
            packed = jnp.where(low, shift(centre, 8 * q, 1), packed)
            packed = jnp.where(high, shift(centre, 8 * q + 8, 1), packed)
        col_send[...] = packed
        for d, (dx, dy) in enumerate(steps):

            @pl.when(inside(dx, dy))
            def _(d=d):
                halo_copy(d, par).start()

        for d, (dx, dy) in enumerate(steps):

            @pl.when(inside(-dx, -dy))
            def _(d=d):
                halo_copy(d, par).wait_recv()

        upper = iota((ROWS, cells_y), 0) < SUB
        ends = [
            jnp.where(upper, corner_recv[par, 0], corner_recv[par, 2]),
            jnp.where(upper, corner_recv[par, 1], corner_recv[par, 3]),
        ]
        east = jnp.concatenate([col_recv[par, 0], ends[0]], axis=0)
        west = jnp.concatenate([col_recv[par, 1], ends[1]], axis=0)
        lane = iota((ext_x, cells_y), 1)
        wide = []
        for q, centre in enumerate(centres):
            end = jnp.where(upper, row_recv[par, 1, q], row_recv[par, 0, q])
            side = jnp.where(lane >= cells_y - SUB, shift(west, -8 * q - 8, 1), 0.0)
            side = jnp.where(lane < SUB, shift(east, -8 * q, 1), side)
            middle = jnp.concatenate([centre, end], axis=0)
            wide.append(jnp.where(keep, jnp.concatenate([middle, side], axis=1), 0.0))
        for c in range(comps):
            state[c] = wide[c]
            load[c] = wide[comps + c]
        coef = wide[2 * comps]

        @pl.when((t == 0) & (group == 0))
        def _():
            for k, (amount, axis) in enumerate(((-1, 0), (1, 0), (-1, 1), (1, 1))):
                stat[k] = 0.5 * (coef + shift(coef, amount, axis))

        @pl.when((t == 0) & (group == 1))
        def _():
            stat[0] = coef
            north = shift(coef, 1, 0)
            west_coef = shift(coef, 1, 1)
            corner = shift(north, 1, 1)
            for c in range(comps):
                total = 0.0
                for node, near_coef in enumerate((coef, north, west_coef, corner)):
                    k = node * comps + c
                    total = total + element_ref[k, k] * near_coef
                stat[1 + c] = RELAX / jnp.where(keep, total, 1.0)

        @pl.when(group == 0)
        def _():
            def sweep(i, carry):
                for c in range(comps):
                    v = state[c]
                    flux = load[c]
                    for k, (amount, axis) in enumerate(((-1, 0), (1, 0), (-1, 1), (1, 1))):
                        flux = flux + stat[k] * (shift(v, amount, axis) - v)
                    state[c] = jnp.where(keep, v + DT_STEP * flux, 0.0)
                return carry

            lax.fori_loop(0, SUB, sweep, 0)

        @pl.when(group == 1)
        def _():
            def sweep(i, carry):
                own = [state[c] for c in range(comps)]
                south = [shift(u, -1, 0) for u in own]
                nodal = own + south
                nodal = nodal + [shift(u, -1, 1) for u in own] + [shift(u, -1, 1) for u in south]
                stiffness = stat[0]

                def force(a):
                    total = element_ref[a, 0] * nodal[0]
                    for b in range(1, 4 * comps):
                        total = total + element_ref[a, b] * nodal[b]
                    return total * stiffness

                for c in range(comps):
                    here = force(c) + shift(force(comps + c), 1, 0)
                    there = force(2 * comps + c) + shift(force(3 * comps + c), 1, 0)
                    total = here + shift(there, 1, 1)
                    result = own[c] + (load[c] - total) * stat[1 + c]
                    state[c] = jnp.where(keep, result, 0.0)
                return carry

            lax.fori_loop(0, SUB, sweep, 0)

        table = jnp.concatenate([state[c, :cells_x, :cells_y] for c in range(comps)], axis=0)
        table = table.astype(BF16)

        def pick(i, carry):
            at = pl.multiple_of(i * ROWS, ROWS)
            source = flat_rows(source_ref[0, pl.ds(at, ROWS), :])
            span = ROWS * width
            columns = one_hot(iota((cells_y, span), 0) == source % cells_y)
            values = jnp.dot(table, columns, preferred_element_type=F32)
            in_row = iota((cells_x, span), 0) == source // cells_y
            parts_of = []
            for c in range(comps):
                chosen = jnp.where(in_row, values[c * cells_x : (c + 1) * cells_x], 0.0)
                total = chosen[:ROWS]
                for r in range(ROWS, cells_x, ROWS):
                    total = total + chosen[r : r + ROWS]
                parts_of.append(total)
            for k in range(ROWS):
                lanes = slice(k * width, (k + 1) * width)
                read = jnp.concatenate([part[:, lanes] for part in parts_of], axis=0)
                mapped = jnp.dot(read.astype(BF16), map_ref[0, at + k], preferred_element_type=F32)
                row = pl.multiple_of((at + k) * ROWS, ROWS)
                for c in range(comps):
                    spread[c, pl.ds(row, ROWS), :] = mapped[c * ROWS : (c + 1) * ROWS]
            return carry

        lax.fori_loop(0, links // ROWS, pick, 0)

        for c in range(comps):
            valued = jnp.dot(slot_map[...], spread[c].astype(BF16), preferred_element_type=F32)
            value_send[:, c] = valued.reshape(parts, ROWS, width)

        def send_value(k, carry):
            value_copy(lax.rem(me + k, parts), me, par).start()
            return carry

        lax.fori_loop(0, parts, send_value, 0)

        for d, (dx, dy) in enumerate(steps):

            @pl.when(inside(dx, dy))
            def _(d=d):
                halo_copy(d, par).wait_send()

        @pl.when(t == 0)
        def _():
            def take(k, carry):
                owner = lax.rem(me - k + parts, parts)
                index_copy(owner, owner).wait_recv()
                return carry

            lax.fori_loop(0, parts, take, 0)

        def place(k, total):
            owner = lax.rem(me - k + parts, parts)
            value_copy(owner, owner, par).wait_recv()
            where = flat_rows(index_recv[owner].astype(jnp.int32))
            span = ROWS * width
            columns = one_hot(iota((cells_y, span), 0) == where % cells_y)
            in_row = iota((cells_x, span), 0) == where // cells_y
            weighted = jnp.concatenate(
                [
                    jnp.where(in_row, flat_rows(value_recv[par, owner, c]), 0.0)
                    for c in range(comps)
                ],
                axis=0,
            ).astype(BF16)
            return total + lax.dot_general(
                weighted, columns, (((1,), (1,)), ((), ())), preferred_element_type=F32
            )

        applied = lax.fori_loop(0, parts, place, jnp.zeros((comps * cells_x, cells_y), F32))
        for c in range(comps):
            part = applied[c * cells_x : (c + 1) * cells_x]
            load_out[0, c] = part
            load[c, :cells_x, :cells_y] = force_ref[0, c] + part

        def sent(k, carry):
            value_copy(lax.rem(me + k, parts), me, par).wait_send()
            return carry

        lax.fori_loop(0, parts, sent, 0)
        return carry

    lax.fori_loop(0, ITERS, coupling, 0)

    def index_sent(k, carry):
        index_copy(lax.rem(me + k, parts), me).wait_send()
        return carry

    lax.fori_loop(0, parts, index_sent, 0)
    for c in range(comps):
        field_out[0, c] = state[c, :cells_x, :cells_y]


def body(parts_x, parts_y, fields, *rest):
    _, comps, cells_x, cells_y = fields.shape
    links, width = rest[3].shape[1:]
    parts = parts_x * parts_y
    ext = (cells_x + ROWS, cells_y + LANES)
    arrays = 2 * comps + 1
    vmem = pl.BlockSpec(memory_space=pltpu.VMEM)
    dma = pltpu.SemaphoreType.DMA
    return pl.pallas_call(
        functools.partial(kernel, parts_x, parts_y),
        out_shape=(jax.ShapeDtypeStruct(fields.shape, F32),) * 2,
        in_specs=[vmem] * 3 + [pl.BlockSpec(memory_space=pltpu.SMEM)] + [vmem] * 4,
        out_specs=(vmem, vmem),
        scratch_shapes=[
            pltpu.VMEM((comps, *ext), F32),
            pltpu.VMEM((comps, *ext), F32),
            pltpu.VMEM((4, *ext), F32),
            pltpu.VMEM((2, arrays, ROWS, cells_y), F32),
            pltpu.VMEM((cells_x, cells_y), F32),
            pltpu.VMEM((2, 2, arrays, ROWS, cells_y), F32),
            pltpu.VMEM((2, 2, cells_x, cells_y), F32),
            pltpu.VMEM((2, 4, ROWS, cells_y), F32),
            pltpu.VMEM((comps, links * ROWS, width), F32),
            pltpu.VMEM((parts * ROWS, links * ROWS), BF16),
            pltpu.VMEM((parts, comps, ROWS, width), F32),
            pltpu.VMEM((2, parts, comps, ROWS, width), F32),
            pltpu.VMEM((parts, ROWS, width), F32),
            pltpu.VMEM((parts, ROWS, width), F32),
            dma((8,)),
            dma((2, 8)),
            dma((parts,)),
            dma((2, parts)),
            dma((parts,)),
            dma((parts,)),
        ],
        compiler_params=pltpu.CompilerParams(collective_id=0, has_side_effects=True),
    )(fields, *rest)


def solution(mesh):
    placed = (
        P("grp", None, "gx", "gy"),
        P("grp", "gx", "gy"),
        P("grp", None, "gx", "gy"),
        P(),
        P("grp", ("gx", "gy"), None),
        P("grp", ("gx", "gy"), None),
        P("grp", ("gx", "gy"), None),
        P("grp", ("gx", "gy"), None, None),
    )
    return jax.shard_map(
        functools.partial(body, mesh.shape["gx"], mesh.shape["gy"]),
        mesh=mesh,
        in_specs=placed,
        out_specs=(P("grp", None, "gx", "gy"), P("grp", None, "gx", "gy")),
        check_vma=False,
    )
```

```python
import functools

import jax
import jax.numpy as jnp
from jax import lax
from jax.experimental import pallas as pl
from jax.experimental.pallas import tpu as pltpu
from jax.sharding import PartitionSpec as P

ITERS = 4
SUB = 4
DT_STEP = 1.0
RELAX = 0.6
ROWS = 8
LANES = 128
F32 = jnp.float32
BF16 = jnp.bfloat16


def iota(shape, dim):
    return lax.broadcasted_iota(jnp.int32, shape, dim)


def shift(value, amount, axis):
    return pltpu.roll(value, amount % value.shape[axis], axis)


def one_hot(mask):
    return jnp.where(mask, 1.0, 0.0).astype(BF16)


def flat_rows(block):
    return jnp.concatenate([block[k : k + 1] for k in range(block.shape[0])], axis=1)


def kernel(
    parts_x,
    parts_y,
    field_ref,
    coef_ref,
    force_ref,
    element_ref,
    source_ref,
    target_ref,
    peer_ref,
    map_hbm,
    field_out,
    load_out,
    state,
    load,
    stat,
    row_send,
    col_send,
    row_recv,
    col_recv,
    corner_recv,
    spread,
    slot_map,
    value_send,
    value_recv,
    index_send,
    index_recv,
    halo_ss,
    halo_rs,
    value_ss,
    value_rs,
    index_ss,
    index_rs,
    map_ref,
    map_sem,
    pick_cols,
    place_cols,
):
    comps, cells_x, cells_y = field_ref.shape[1:]
    links, width = source_ref.shape[1:]
    parts = parts_x * parts_y
    slots = parts * ROWS
    ext_x, ext_y = state.shape[1:]
    group = lax.axis_index("grp")
    gx = lax.axis_index("gx")
    gy = lax.axis_index("gy")
    me = gx * parts_y + gy

    def peer_device(q):
        return {"grp": 1 - group, "gx": lax.div(q, parts_y), "gy": lax.rem(q, parts_y)}

    def inside(dx, dy):
        ok = None
        for pos, step, size in ((gx, dx, parts_x), (gy, dy, parts_y)):
            if step:
                test = (pos + step >= 0) & (pos + step < size)
                ok = test if ok is None else ok & test
        return ok

    steps = ((1, 0), (-1, 0), (0, -1), (0, 1), (-1, -1), (-1, 1), (1, -1), (1, 1))

    row_send[...] = jnp.zeros_like(row_send)
    col_send[...] = jnp.zeros_like(col_send)
    row_recv[...] = jnp.zeros_like(row_recv)
    col_recv[...] = jnp.zeros_like(col_recv)
    corner_recv[...] = jnp.zeros_like(corner_recv)

    barrier = pltpu.get_barrier_semaphore()

    def greet(k, carry):
        q = lax.rem(me + k, parts)
        pl.semaphore_signal(
            barrier, inc=1, device_id=peer_device(q), device_id_type=pl.DeviceIdType.MESH
        )
        return carry

    lax.fori_loop(0, parts, greet, 0)
    for dx, dy in steps:

        @pl.when(inside(dx, dy))
        def _(dx=dx, dy=dy):
            pl.semaphore_signal(
                barrier,
                inc=1,
                device_id={"gx": gx + dx, "gy": gy + dy},
                device_id_type=pl.DeviceIdType.MESH,
            )

    pltpu.make_async_copy(map_hbm, map_ref, map_sem).start()
    peer_row = jnp.broadcast_to(peer_ref[0].astype(F32), (links, links))
    above, across = iota((links, links), 0), iota((links, links), 1)
    peer_col = jnp.sum(jnp.where(above == across, peer_row, 0.0), axis=1, keepdims=True)
    rank = jnp.sum(
        jnp.where((peer_col == peer_row) & (above < across), 1.0, 0.0), axis=0, keepdims=True
    )
    slot_row = (peer_row[:1] * ROWS + rank).astype(jnp.int32)
    to_slot = one_hot(iota((slots, links), 0) == slot_row)
    repeat = one_hot(iota((links, links * ROWS), 0) == iota((links, links * ROWS), 1) // ROWS)
    slot_map[...] = jnp.dot(to_slot, repeat, preferred_element_type=F32).astype(BF16)
    target = target_ref[0]
    target_x = (target // cells_y).astype(F32).astype(BF16)
    target_y = (target % cells_y).astype(F32).astype(BF16)
    index = cells_y * jnp.dot(to_slot, target_x, preferred_element_type=F32)
    index = index + jnp.dot(to_slot, target_y, preferred_element_type=F32)
    index_send[...] = index.reshape(parts, ROWS, width)

    def index_copy(q, owner):
        return pltpu.make_async_remote_copy(
            src_ref=index_send.at[q],
            dst_ref=index_recv.at[owner],
            send_sem=index_ss.at[q],
            recv_sem=index_rs.at[owner],
            device_id=peer_device(q),
            device_id_type=pl.DeviceIdType.MESH,
        )

    def value_copy(q, owner, par):
        return pltpu.make_async_remote_copy(
            src_ref=value_send.at[q],
            dst_ref=value_recv.at[par, owner],
            send_sem=value_ss.at[q],
            recv_sem=value_rs.at[par, owner],
            device_id=peer_device(q),
            device_id_type=pl.DeviceIdType.MESH,
        )

    def halo_copy(d, par):
        dx, dy = steps[d]
        if d < 2:
            source, place = row_send.at[1 - d], row_recv.at[par, d]
        elif d < 4:
            source, place = col_send, col_recv.at[par, d - 2]
        else:
            edge = pl.ds(0, ROWS) if d < 6 else pl.ds(cells_x - ROWS, ROWS)
            source, place = col_send.at[edge], corner_recv.at[par, d - 4]
        return pltpu.make_async_remote_copy(
            src_ref=source,
            dst_ref=place,
            send_sem=halo_ss.at[d],
            recv_sem=halo_rs.at[par, d],
            device_id={"gx": gx + dx, "gy": gy + dy},
            device_id_type=pl.DeviceIdType.MESH,
        )

    span = ROWS * width

    def prepare(i, carry):
        at = pl.multiple_of(i * ROWS, ROWS)
        source = flat_rows(source_ref[0, pl.ds(at, ROWS), :])
        pick_cols[i] = one_hot(iota((cells_y, span), 0) == source % cells_y)
        return carry

    lax.fori_loop(0, links // ROWS, prepare, 0)

    beside_x = jnp.where(gx > 0, 1, 0) + jnp.where(gx < parts_x - 1, 1, 0)
    beside_y = jnp.where(gy > 0, 1, 0) + jnp.where(gy < parts_y - 1, 1, 0)
    pl.semaphore_wait(barrier, parts + (beside_x + 1) * (beside_y + 1) - 1)

    def send_index(k, carry):
        index_copy(lax.rem(me + k, parts), me).start()
        return carry

    lax.fori_loop(0, parts, send_index, 0)

    for c in range(comps):
        state[c, :cells_x, :cells_y] = field_ref[0, c]
        load[c, :cells_x, :cells_y] = force_ref[0, c]

    ext_row = iota((ext_x, ext_y), 0)
    ext_col = iota((ext_x, ext_y), 1)
    row_at = jnp.where(ext_row < cells_x + SUB, ext_row, ext_row - ext_x) + gx * cells_x
    near = (ext_col < cells_y + SUB) | (ext_col >= ext_y - SUB)
    col_at = jnp.where(ext_col < cells_y + SUB, ext_col, ext_col - ext_y) + gy * cells_y
    keep = near & (row_at >= 0) & (row_at < cells_x * parts_x)
    keep = keep & (col_at >= 0) & (col_at < cells_y * parts_y)

    def coupling(t, carry):
        par = lax.rem(t, 2)
        centres = [state[c, :cells_x, :cells_y] for c in range(comps)]
        centres += [load[c, :cells_x, :cells_y] for c in range(comps)]
        centres.append(coef_ref[0])
        lane = iota((cells_x, cells_y), 1)
        packed = jnp.zeros((cells_x, cells_y), F32)
        for q, centre in enumerate(centres):
            row_send[0, q] = centre[:ROWS]
            row_send[1, q] = centre[cells_x - ROWS :]
            low = (lane >= 8 * q) & (lane < 8 * q + 4)
            high = (lane >= 8 * q + 4) & (lane < 8 * q + 8)
            packed = jnp.where(low, shift(centre, 8 * q, 1), packed)
            packed = jnp.where(high, shift(centre, 8 * q + 8, 1), packed)
        col_send[...] = packed
        for d, (dx, dy) in enumerate(steps):

            @pl.when(inside(dx, dy))
            def _(d=d):
                halo_copy(d, par).start()

        for d, (dx, dy) in enumerate(steps):

            @pl.when(inside(-dx, -dy))
            def _(d=d):
                halo_copy(d, par).wait_recv()

        upper = iota((ROWS, cells_y), 0) < SUB
        ends = [
            jnp.where(upper, corner_recv[par, 0], corner_recv[par, 2]),
            jnp.where(upper, corner_recv[par, 1], corner_recv[par, 3]),
        ]
        east = jnp.concatenate([col_recv[par, 0], ends[0]], axis=0)
        west = jnp.concatenate([col_recv[par, 1], ends[1]], axis=0)
        lane = iota((ext_x, cells_y), 1)
        wide = []
        for q, centre in enumerate(centres):
            end = jnp.where(upper, row_recv[par, 1, q], row_recv[par, 0, q])
            side = jnp.where(lane >= cells_y - SUB, shift(west, -8 * q - 8, 1), 0.0)
            side = jnp.where(lane < SUB, shift(east, -8 * q, 1), side)
            middle = jnp.concatenate([centre, end], axis=0)
            wide.append(jnp.where(keep, jnp.concatenate([middle, side], axis=1), 0.0))
        for c in range(comps):
            state[c] = wide[c]
            load[c] = wide[comps + c]
        coef = wide[2 * comps]

        @pl.when((t == 0) & (group == 0))
        def _():
            for k, (amount, axis) in enumerate(((-1, 0), (1, 0), (-1, 1), (1, 1))):
                stat[k] = 0.5 * (coef + shift(coef, amount, axis))

        @pl.when((t == 0) & (group == 1))
        def _():
            stat[0] = coef
            north = shift(coef, 1, 0)
            west_coef = shift(coef, 1, 1)
            corner = shift(north, 1, 1)
            for c in range(comps):
                total = 0.0
                for node, near_coef in enumerate((coef, north, west_coef, corner)):
                    k = node * comps + c
                    total = total + element_ref[k, k] * near_coef
                stat[1 + c] = RELAX / jnp.where(keep, total, 1.0)

        @pl.when(group == 0)
        def _():
            def sweep(i, carry):
                for c in range(comps):
                    v = state[c]
                    flux = load[c]
                    for k, (amount, axis) in enumerate(((-1, 0), (1, 0), (-1, 1), (1, 1))):
                        flux = flux + stat[k] * (shift(v, amount, axis) - v)
                    state[c] = jnp.where(keep, v + DT_STEP * flux, 0.0)
                return carry

            lax.fori_loop(0, SUB, sweep, 0)

        @pl.when(group == 1)
        def _():
            def sweep(i, carry):
                own = [state[c] for c in range(comps)]
                south = [shift(u, -1, 0) for u in own]
                nodal = own + south
                nodal = nodal + [shift(u, -1, 1) for u in own] + [shift(u, -1, 1) for u in south]
                stiffness = stat[0]

                def force(a):
                    total = element_ref[a, 0] * nodal[0]
                    for b in range(1, 4 * comps):
                        total = total + element_ref[a, b] * nodal[b]
                    return total * stiffness

                for c in range(comps):
                    here = force(c) + shift(force(comps + c), 1, 0)
                    there = force(2 * comps + c) + shift(force(3 * comps + c), 1, 0)
                    total = here + shift(there, 1, 1)
                    result = own[c] + (load[c] - total) * stat[1 + c]
                    state[c] = jnp.where(keep, result, 0.0)
                return carry

            lax.fori_loop(0, SUB, sweep, 0)

        @pl.when(t == 0)
        def _():
            pltpu.make_async_copy(map_hbm, map_ref, map_sem).wait()

        table = jnp.concatenate([state[c, :cells_x, :cells_y] for c in range(comps)], axis=0)
        table = table.astype(BF16)

        def pick(i, carry):
            at = pl.multiple_of(i * ROWS, ROWS)
            source = flat_rows(source_ref[0, pl.ds(at, ROWS), :])
            values = jnp.dot(table, pick_cols[i], preferred_element_type=F32)
            in_row = iota((cells_x, span), 0) == source // cells_y
            parts_of = []
            for c in range(comps):
                chosen = jnp.where(in_row, values[c * cells_x : (c + 1) * cells_x], 0.0)
                total = chosen[:ROWS]
                for r in range(ROWS, cells_x, ROWS):
                    total = total + chosen[r : r + ROWS]
                parts_of.append(total)
            for k in range(ROWS):
                lanes = slice(k * width, (k + 1) * width)
                read = jnp.concatenate([part[:, lanes] for part in parts_of], axis=0)
                mapped = jnp.dot(read.astype(BF16), map_ref[0, at + k], preferred_element_type=F32)
                row = pl.multiple_of((at + k) * ROWS, ROWS)
                for c in range(comps):
                    spread[c, pl.ds(row, ROWS), :] = mapped[c * ROWS : (c + 1) * ROWS]
            return carry

        lax.fori_loop(0, links // ROWS, pick, 0, unroll=4)

        for c in range(comps):
            valued = jnp.dot(slot_map[...], spread[c].astype(BF16), preferred_element_type=F32)
            value_send[:, c] = valued.reshape(parts, ROWS, width)

        def send_value(k, carry):
            value_copy(lax.rem(me + k, parts), me, par).start()
            return carry

        lax.fori_loop(0, parts, send_value, 0)

        for d, (dx, dy) in enumerate(steps):

            @pl.when(inside(dx, dy))
            def _(d=d):
                halo_copy(d, par).wait_send()

        @pl.when(t == 0)
        def _():
            def take(k, carry):
                owner = lax.rem(me - k + parts, parts)
                index_copy(owner, owner).wait_recv()
                where = flat_rows(index_recv[owner].astype(jnp.int32))
                mask = jnp.where(iota((cells_y, span), 0) == where % cells_y, 1.0, 0.0)
                place_cols[owner] = mask.T.astype(BF16)
                return carry

            lax.fori_loop(0, parts, take, 0)

        def place(k, total):
            owner = lax.rem(me - k + parts, parts)
            value_copy(owner, owner, par).wait_recv()
            where = flat_rows(index_recv[owner].astype(jnp.int32))
            in_row = iota((cells_x, span), 0) == where // cells_y
            weighted = jnp.concatenate(
                [
                    jnp.where(in_row, flat_rows(value_recv[par, owner, c]), 0.0)
                    for c in range(comps)
                ],
                axis=0,
            ).astype(BF16)
            return total + lax.dot_general(
                weighted, place_cols[owner], (((1,), (0,)), ((), ())), preferred_element_type=F32
            )

        applied = lax.fori_loop(0, parts, place, jnp.zeros((comps * cells_x, cells_y), F32), unroll=4)
        for c in range(comps):
            part = applied[c * cells_x : (c + 1) * cells_x]
            load_out[0, c] = part
            load[c, :cells_x, :cells_y] = force_ref[0, c] + part

        def sent(k, carry):
            value_copy(lax.rem(me + k, parts), me, par).wait_send()
            return carry

        lax.fori_loop(0, parts, sent, 0)
        return carry

    lax.fori_loop(0, ITERS, coupling, 0)

    def index_sent(k, carry):
        index_copy(lax.rem(me + k, parts), me).wait_send()
        return carry

    lax.fori_loop(0, parts, index_sent, 0)
    for c in range(comps):
        field_out[0, c] = state[c, :cells_x, :cells_y]


def hand_over(field_ref, load_ref, field_out, load_out):
    field_out[...] = field_ref[...]
    load_out[...] = load_ref[...]


def body(parts_x, parts_y, fields, *rest):
    _, comps, cells_x, cells_y = fields.shape
    links, width = rest[3].shape[1:]
    parts = parts_x * parts_y
    ext = (cells_x + ROWS, cells_y + LANES)
    arrays = 2 * comps + 1
    vmem = pl.BlockSpec(memory_space=pltpu.VMEM)
    dma = pltpu.SemaphoreType.DMA
    rest = (*rest[:5], rest[5].reshape(1, 1, links), rest[6])
    results = pl.pallas_call(
        functools.partial(kernel, parts_x, parts_y),
        out_shape=(jax.ShapeDtypeStruct(fields.shape, F32),) * 2,
        in_specs=[vmem] * 3 + [pl.BlockSpec(memory_space=pltpu.SMEM)] + [vmem] * 3
        + [pl.BlockSpec(memory_space=pl.ANY)],
        out_specs=(vmem, vmem),
        scratch_shapes=[
            pltpu.VMEM((comps, *ext), F32),
            pltpu.VMEM((comps, *ext), F32),
            pltpu.VMEM((4, *ext), F32),
            pltpu.VMEM((2, arrays, ROWS, cells_y), F32),
            pltpu.VMEM((cells_x, cells_y), F32),
            pltpu.VMEM((2, 2, arrays, ROWS, cells_y), F32),
            pltpu.VMEM((2, 2, cells_x, cells_y), F32),
            pltpu.VMEM((2, 4, ROWS, cells_y), F32),
            pltpu.VMEM((comps, links * ROWS, width), F32),
            pltpu.VMEM((parts * ROWS, links * ROWS), BF16),
            pltpu.VMEM((parts, comps, ROWS, width), F32),
            pltpu.VMEM((2, parts, comps, ROWS, width), F32),
            pltpu.VMEM((parts, ROWS, width), F32),
            pltpu.VMEM((parts, ROWS, width), F32),
            dma((8,)),
            dma((2, 8)),
            dma((parts,)),
            dma((2, parts)),
            dma((parts,)),
            dma((parts,)),
            pltpu.VMEM(rest[6].shape, BF16),
            dma,
            pltpu.VMEM((links // ROWS, cells_y, ROWS * width), BF16),
            pltpu.VMEM((parts, ROWS * width, cells_y), BF16),
        ],
        compiler_params=pltpu.CompilerParams(collective_id=0, has_side_effects=True),
    )(fields, *rest)
    return pl.pallas_call(
        hand_over, out_shape=(jax.ShapeDtypeStruct(fields.shape, F32),) * 2, in_specs=[vmem] * 2, out_specs=(vmem, vmem)
    )(*results)


def solution(mesh):
    placed = (
        P("grp", None, "gx", "gy"),
        P("grp", "gx", "gy"),
        P("grp", None, "gx", "gy"),
        P(),
        P("grp", ("gx", "gy"), None),
        P("grp", ("gx", "gy"), None),
        P("grp", ("gx", "gy"), None),
        P("grp", ("gx", "gy"), None, None),
    )
    return jax.shard_map(
        functools.partial(body, mesh.shape["gx"], mesh.shape["gy"]),
        mesh=mesh,
        in_specs=placed,
        out_specs=(P("grp", None, "gx", "gy"), P("grp", None, "gx", "gy")),
        check_vma=False,
    )
```

```python
import functools

import jax
import jax.numpy as jnp
from jax import lax
from jax.experimental import pallas as pl
from jax.experimental.pallas import tpu as pltpu
from jax.sharding import PartitionSpec as P

ITERS = 4
SUB = 4
DT_STEP = 1.0
RELAX = 0.6
ROWS = 8
LANES = 128
F32 = jnp.float32
BF16 = jnp.bfloat16


def iota(shape, dim):
    return lax.broadcasted_iota(jnp.int32, shape, dim)


def shift(value, amount, axis):
    return pltpu.roll(value, amount % value.shape[axis], axis)


def one_hot(mask):
    return jnp.where(mask, 1.0, 0.0).astype(BF16)


def flat_rows(block):
    return jnp.concatenate([block[k : k + 1] for k in range(block.shape[0])], axis=1)


def kernel(
    parts_x,
    parts_y,
    field_ref,
    coef_ref,
    force_ref,
    element_ref,
    source_ref,
    target_ref,
    peer_ref,
    map_hbm,
    field_out,
    load_out,
    state,
    load,
    stat,
    row_send,
    col_send,
    row_recv,
    col_recv,
    corner_recv,
    spread,
    slot_map,
    value_send,
    value_recv,
    index_send,
    index_recv,
    halo_ss,
    halo_rs,
    value_ss,
    value_rs,
    index_ss,
    index_rs,
    map_ref,
    map_sem,
    pick_cols,
    place_cols,
):
    comps, cells_x, cells_y = field_ref.shape[1:]
    links, width = source_ref.shape[1:]
    parts = parts_x * parts_y
    slots = parts * ROWS
    ext_x, ext_y = state.shape[1:]
    group = lax.axis_index("grp")
    gx = lax.axis_index("gx")
    gy = lax.axis_index("gy")
    me = gx * parts_y + gy

    def peer_device(q):
        return {"grp": 1 - group, "gx": lax.div(q, parts_y), "gy": lax.rem(q, parts_y)}

    halves = 2 if parts_x % 2 == 0 else 1
    half = parts_x // halves

    def partner_of(k, sign, across):
        turn = lax.div(k, half * parts_y)
        turn = halves - 1 - turn if across else turn
        within = lax.rem(k, half * parts_y)
        along = lax.rem(lax.rem(gx, half) + sign * lax.div(within, parts_y) + half, half)
        x = lax.rem(lax.div(gx, half) + turn, halves) * half + along
        y = lax.rem(gy + sign * lax.rem(within, parts_y) + parts_y, parts_y)
        return x * parts_y + y

    def inside(dx, dy):
        ok = None
        for pos, step, size in ((gx, dx, parts_x), (gy, dy, parts_y)):
            if step:
                test = (pos + step >= 0) & (pos + step < size)
                ok = test if ok is None else ok & test
        return ok

    steps = ((1, 0), (-1, 0), (0, -1), (0, 1), (-1, -1), (-1, 1), (1, -1), (1, 1))

    row_send[...] = jnp.zeros_like(row_send)
    col_send[...] = jnp.zeros_like(col_send)
    row_recv[...] = jnp.zeros_like(row_recv)
    col_recv[...] = jnp.zeros_like(col_recv)
    corner_recv[...] = jnp.zeros_like(corner_recv)

    barrier = pltpu.get_barrier_semaphore()

    def greet(k, carry):
        q = lax.rem(me + k, parts)
        pl.semaphore_signal(
            barrier, inc=1, device_id=peer_device(q), device_id_type=pl.DeviceIdType.MESH
        )
        return carry

    lax.fori_loop(0, parts, greet, 0)
    for dx, dy in steps:

        @pl.when(inside(dx, dy))
        def _(dx=dx, dy=dy):
            pl.semaphore_signal(
                barrier,
                inc=1,
                device_id={"gx": gx + dx, "gy": gy + dy},
                device_id_type=pl.DeviceIdType.MESH,
            )

    pltpu.make_async_copy(map_hbm, map_ref, map_sem).start()
    peer_row = jnp.broadcast_to(peer_ref[0].astype(F32), (links, links))
    above, across = iota((links, links), 0), iota((links, links), 1)
    peer_col = jnp.sum(jnp.where(above == across, peer_row, 0.0), axis=1, keepdims=True)
    rank = jnp.sum(
        jnp.where((peer_col == peer_row) & (above < across), 1.0, 0.0), axis=0, keepdims=True
    )
    slot_row = (peer_row[:1] * ROWS + rank).astype(jnp.int32)
    to_slot = one_hot(iota((slots, links), 0) == slot_row)
    repeat = one_hot(iota((links, links * ROWS), 0) == iota((links, links * ROWS), 1) // ROWS)
    slot_map[...] = jnp.dot(to_slot, repeat, preferred_element_type=F32).astype(BF16)
    target = target_ref[0]
    target_x = (target // cells_y).astype(F32).astype(BF16)
    target_y = (target % cells_y).astype(F32).astype(BF16)
    index = cells_y * jnp.dot(to_slot, target_x, preferred_element_type=F32)
    index = index + jnp.dot(to_slot, target_y, preferred_element_type=F32)
    index_send[...] = index.reshape(parts, ROWS, width)

    def index_copy(q, owner):
        return pltpu.make_async_remote_copy(
            src_ref=index_send.at[q],
            dst_ref=index_recv.at[owner],
            send_sem=index_ss.at[q],
            recv_sem=index_rs.at[owner],
            device_id=peer_device(q),
            device_id_type=pl.DeviceIdType.MESH,
        )

    def value_copy(q, owner, par):
        return pltpu.make_async_remote_copy(
            src_ref=value_send.at[q],
            dst_ref=value_recv.at[par, owner],
            send_sem=value_ss.at[q],
            recv_sem=value_rs.at[par, owner],
            device_id=peer_device(q),
            device_id_type=pl.DeviceIdType.MESH,
        )

    def halo_copy(d, par):
        dx, dy = steps[d]
        if d < 2:
            source, place = row_send.at[1 - d], row_recv.at[par, d]
        elif d < 4:
            source, place = col_send, col_recv.at[par, d - 2]
        else:
            edge = pl.ds(0, ROWS) if d < 6 else pl.ds(cells_x - ROWS, ROWS)
            source, place = col_send.at[edge], corner_recv.at[par, d - 4]
        return pltpu.make_async_remote_copy(
            src_ref=source,
            dst_ref=place,
            send_sem=halo_ss.at[d],
            recv_sem=halo_rs.at[par, d],
            device_id={"gx": gx + dx, "gy": gy + dy},
            device_id_type=pl.DeviceIdType.MESH,
        )

    span = ROWS * width

    def prepare(i, carry):
        at = pl.multiple_of(i * ROWS, ROWS)
        source = flat_rows(source_ref[0, pl.ds(at, ROWS), :])
        pick_cols[i] = one_hot(iota((cells_y, span), 0) == source % cells_y)
        return carry

    lax.fori_loop(0, links // ROWS, prepare, 0)

    beside_x = jnp.where(gx > 0, 1, 0) + jnp.where(gx < parts_x - 1, 1, 0)
    beside_y = jnp.where(gy > 0, 1, 0) + jnp.where(gy < parts_y - 1, 1, 0)
    pl.semaphore_wait(barrier, parts + (beside_x + 1) * (beside_y + 1) - 1)

    def send_index(k, carry):
        index_copy(lax.rem(me + k, parts), me).start()
        return carry

    lax.fori_loop(0, parts, send_index, 0)

    for c in range(comps):
        state[c, :cells_x, :cells_y] = field_ref[0, c]
        load[c, :cells_x, :cells_y] = force_ref[0, c]

    ext_row = iota((ext_x, ext_y), 0)
    ext_col = iota((ext_x, ext_y), 1)
    row_at = jnp.where(ext_row < cells_x + SUB, ext_row, ext_row - ext_x) + gx * cells_x
    near = (ext_col < cells_y + SUB) | (ext_col >= ext_y - SUB)
    col_at = jnp.where(ext_col < cells_y + SUB, ext_col, ext_col - ext_y) + gy * cells_y
    keep = near & (row_at >= 0) & (row_at < cells_x * parts_x)
    keep = keep & (col_at >= 0) & (col_at < cells_y * parts_y)

    def coupling(t, carry):
        par = lax.rem(t, 2)
        centres = [state[c, :cells_x, :cells_y] for c in range(comps)]
        centres += [load[c, :cells_x, :cells_y] for c in range(comps)]
        centres.append(coef_ref[0])
        lane = iota((cells_x, cells_y), 1)
        packed = jnp.zeros((cells_x, cells_y), F32)
        for q, centre in enumerate(centres):
            row_send[0, q] = centre[:ROWS]
            row_send[1, q] = centre[cells_x - ROWS :]
            low = (lane >= 8 * q) & (lane < 8 * q + 4)
            high = (lane >= 8 * q + 4) & (lane < 8 * q + 8)
            packed = jnp.where(low, shift(centre, 8 * q, 1), packed)
            packed = jnp.where(high, shift(centre, 8 * q + 8, 1), packed)
        col_send[...] = packed
        for d, (dx, dy) in reversed(list(enumerate(steps))):

            @pl.when(inside(dx, dy))
            def _(d=d):
                halo_copy(d, par).start()

        for d, (dx, dy) in enumerate(steps):

            @pl.when(inside(-dx, -dy))
            def _(d=d):
                halo_copy(d, par).wait_recv()

        upper = iota((ROWS, cells_y), 0) < SUB
        ends = [
            jnp.where(upper, corner_recv[par, 0], corner_recv[par, 2]),
            jnp.where(upper, corner_recv[par, 1], corner_recv[par, 3]),
        ]
        east = jnp.concatenate([col_recv[par, 0], ends[0]], axis=0)
        west = jnp.concatenate([col_recv[par, 1], ends[1]], axis=0)
        lane = iota((ext_x, cells_y), 1)
        wide = []
        for q, centre in enumerate(centres):
            end = jnp.where(upper, row_recv[par, 1, q], row_recv[par, 0, q])
            side = jnp.where(lane >= cells_y - SUB, shift(west, -8 * q - 8, 1), 0.0)
            side = jnp.where(lane < SUB, shift(east, -8 * q, 1), side)
            middle = jnp.concatenate([centre, end], axis=0)
            wide.append(jnp.where(keep, jnp.concatenate([middle, side], axis=1), 0.0))
        for c in range(comps):
            state[c] = wide[c]
            load[c] = wide[comps + c]
        coef = wide[2 * comps]

        @pl.when((t == 0) & (group == 0))
        def _():
            for k, (amount, axis) in enumerate(((-1, 0), (1, 0), (-1, 1), (1, 1))):
                stat[k] = 0.5 * (coef + shift(coef, amount, axis))

        @pl.when((t == 0) & (group == 1))
        def _():
            stat[0] = coef
            north = shift(coef, 1, 0)
            west_coef = shift(coef, 1, 1)
            corner = shift(north, 1, 1)
            for c in range(comps):
                total = 0.0
                for node, near_coef in enumerate((coef, north, west_coef, corner)):
                    k = node * comps + c
                    total = total + element_ref[k, k] * near_coef
                stat[1 + c] = RELAX / jnp.where(keep, total, 1.0)

        @pl.when(group == 0)
        def _():
            def sweep(i, carry):
                for c in range(comps):
                    v = state[c]
                    flux = load[c]
                    for k, (amount, axis) in enumerate(((-1, 0), (1, 0), (-1, 1), (1, 1))):
                        flux = flux + stat[k] * (shift(v, amount, axis) - v)
                    state[c] = jnp.where(keep, v + DT_STEP * flux, 0.0)
                return carry

            lax.fori_loop(0, SUB, sweep, 0, unroll=True)

        @pl.when(group == 1)
        def _():
            def sweep(i, carry):
                own = [state[c] for c in range(comps)]
                south = [shift(u, -1, 0) for u in own]
                nodal = own + south
                nodal = nodal + [shift(u, -1, 1) for u in own] + [shift(u, -1, 1) for u in south]
                stiffness = stat[0]

                def force(a):
                    total = element_ref[a, 0] * nodal[0]
                    for b in range(1, 4 * comps):
                        total = total + element_ref[a, b] * nodal[b]
                    return total * stiffness

                for c in range(comps):
                    here = force(c) + shift(force(comps + c), 1, 0)
                    there = force(2 * comps + c) + shift(force(3 * comps + c), 1, 0)
                    total = here + shift(there, 1, 1)
                    result = own[c] + (load[c] - total) * stat[1 + c]
                    state[c] = jnp.where(keep, result, 0.0)
                return carry

            lax.fori_loop(0, SUB, sweep, 0, unroll=True)

        @pl.when(t == 0)
        def _():
            pltpu.make_async_copy(map_hbm, map_ref, map_sem).wait()

        table = jnp.concatenate([state[c, :cells_x, :cells_y] for c in range(comps)], axis=0)
        table = table.astype(BF16)

        def pick(i, carry):
            at = pl.multiple_of(i * ROWS, ROWS)
            source = flat_rows(source_ref[0, pl.ds(at, ROWS), :])
            values = jnp.dot(table, pick_cols[i], preferred_element_type=F32)
            in_row = iota((cells_x, span), 0) == source // cells_y
            parts_of = []
            for c in range(comps):
                chosen = jnp.where(in_row, values[c * cells_x : (c + 1) * cells_x], 0.0)
                total = chosen[:ROWS]
                for r in range(ROWS, cells_x, ROWS):
                    total = total + chosen[r : r + ROWS]
                parts_of.append(total)
            for k in range(ROWS):
                lanes = slice(k * width, (k + 1) * width)
                read = jnp.concatenate([part[:, lanes] for part in parts_of], axis=0)
                mapped = jnp.dot(read.astype(BF16), map_ref[0, at + k], preferred_element_type=F32)
                row = pl.multiple_of((at + k) * ROWS, ROWS)
                for c in range(comps):
                    spread[c, pl.ds(row, ROWS), :] = mapped[c * ROWS : (c + 1) * ROWS]
            return carry

        lax.fori_loop(0, links // ROWS, pick, 0, unroll=4)

        for c in range(comps):
            valued = jnp.dot(slot_map[...], spread[c].astype(BF16), preferred_element_type=F32)
            value_send[:, c] = valued.reshape(parts, ROWS, width)

        def send_value(k, carry):
            value_copy(partner_of(k, 1, True), me, par).start()
            return carry

        lax.fori_loop(0, parts, send_value, 0, unroll=4)

        for d, (dx, dy) in enumerate(steps):

            @pl.when(inside(dx, dy))
            def _(d=d):
                halo_copy(d, par).wait_send()

        @pl.when(t == 0)
        def _():
            def take(k, carry):
                owner = lax.rem(me - k + parts, parts)
                index_copy(owner, owner).wait_recv()
                where = flat_rows(index_recv[owner].astype(jnp.int32))
                mask = jnp.where(iota((cells_y, span), 0) == where % cells_y, 1.0, 0.0)
                place_cols[owner] = mask.T.astype(BF16)
                return carry

            lax.fori_loop(0, parts, take, 0)

        def place(k, total):
            owner = partner_of(k, -1, False)
            value_copy(owner, owner, par).wait_recv()
            where = flat_rows(index_recv[owner].astype(jnp.int32))
            in_row = iota((cells_x, span), 0) == where // cells_y
            weighted = jnp.concatenate(
                [
                    jnp.where(in_row, flat_rows(value_recv[par, owner, c]), 0.0)
                    for c in range(comps)
                ],
                axis=0,
            ).astype(BF16)
            return total + lax.dot_general(
                weighted, place_cols[owner], (((1,), (0,)), ((), ())), preferred_element_type=F32
            )

        applied = lax.fori_loop(0, parts, place, jnp.zeros((comps * cells_x, cells_y), F32), unroll=4)
        for c in range(comps):
            part = applied[c * cells_x : (c + 1) * cells_x]
            load_out[0, c] = part
            load[c, :cells_x, :cells_y] = force_ref[0, c] + part

        def sent(k, carry):
            value_copy(lax.rem(me + k, parts), me, par).wait_send()
            return carry

        lax.fori_loop(0, parts, sent, 0)
        return carry

    lax.fori_loop(0, ITERS, coupling, 0)

    def index_sent(k, carry):
        index_copy(lax.rem(me + k, parts), me).wait_send()
        return carry

    lax.fori_loop(0, parts, index_sent, 0)
    for c in range(comps):
        field_out[0, c] = state[c, :cells_x, :cells_y]


def hand_over(field_ref, load_ref, field_out, load_out):
    field_out[...] = field_ref[...]
    load_out[...] = load_ref[...]


def body(parts_x, parts_y, fields, *rest):
    _, comps, cells_x, cells_y = fields.shape
    links, width = rest[3].shape[1:]
    parts = parts_x * parts_y
    ext = (cells_x + ROWS, cells_y + LANES)
    arrays = 2 * comps + 1
    vmem = pl.BlockSpec(memory_space=pltpu.VMEM)
    dma = pltpu.SemaphoreType.DMA
    rest = (*rest[:5], rest[5].reshape(1, 1, links), rest[6])
    results = pl.pallas_call(
        functools.partial(kernel, parts_x, parts_y),
        out_shape=(jax.ShapeDtypeStruct(fields.shape, F32),) * 2,
        in_specs=[vmem] * 3 + [pl.BlockSpec(memory_space=pltpu.SMEM)] + [vmem] * 3
        + [pl.BlockSpec(memory_space=pl.ANY)],
        out_specs=(vmem, vmem),
        scratch_shapes=[
            pltpu.VMEM((comps, *ext), F32),
            pltpu.VMEM((comps, *ext), F32),
            pltpu.VMEM((4, *ext), F32),
            pltpu.VMEM((2, arrays, ROWS, cells_y), F32),
            pltpu.VMEM((cells_x, cells_y), F32),
            pltpu.VMEM((2, 2, arrays, ROWS, cells_y), F32),
            pltpu.VMEM((2, 2, cells_x, cells_y), F32),
            pltpu.VMEM((2, 4, ROWS, cells_y), F32),
            pltpu.VMEM((comps, links * ROWS, width), F32),
            pltpu.VMEM((parts * ROWS, links * ROWS), BF16),
            pltpu.VMEM((parts, comps, ROWS, width), F32),
            pltpu.VMEM((2, parts, comps, ROWS, width), F32),
            pltpu.VMEM((parts, ROWS, width), F32),
            pltpu.VMEM((parts, ROWS, width), F32),
            dma((8,)),
            dma((2, 8)),
            dma((parts,)),
            dma((2, parts)),
            dma((parts,)),
            dma((parts,)),
            pltpu.VMEM(rest[6].shape, BF16),
            dma,
            pltpu.VMEM((links // ROWS, cells_y, ROWS * width), BF16),
            pltpu.VMEM((parts, ROWS * width, cells_y), BF16),
        ],
        compiler_params=pltpu.CompilerParams(collective_id=0, has_side_effects=True),
    )(fields, *rest)
    return pl.pallas_call(
        hand_over, out_shape=(jax.ShapeDtypeStruct(fields.shape, F32),) * 2, in_specs=[vmem] * 2, out_specs=(vmem, vmem)
    )(*results)


def solution(mesh):
    placed = (
        P("grp", None, "gx", "gy"),
        P("grp", "gx", "gy"),
        P("grp", None, "gx", "gy"),
        P(),
        P("grp", ("gx", "gy"), None),
        P("grp", ("gx", "gy"), None),
        P("grp", ("gx", "gy"), None),
        P("grp", ("gx", "gy"), None, None),
    )
    return jax.shard_map(
        functools.partial(body, mesh.shape["gx"], mesh.shape["gy"]),
        mesh=mesh,
        in_specs=placed,
        out_specs=(P("grp", None, "gx", "gy"), P("grp", None, "gx", "gy")),
        check_vma=False,
    )
```
